32 devices in a mesh: layer: 4 (over y, core), feat: 8 (over z, x).
Axes of the slice: x: 2, y: 2, z: 4, core: 2. Of those that a mesh axis runs over, the one named last changes fastest.
Arguments:
- acts: bfloat16 [4, 768, 1024], P('layer'), may hold values from -6 to 6
- targets: bfloat16 [4, 768, 1024], P('layer', 'feat'), may hold values from -6 to 6
- enc_weight: bfloat16 [4, 1024, 20480], P('layer', None, 'feat'), may hold values from -0.1875 to 0.1875
- enc_bias: float32 [4, 20480], P('layer', 'feat'), may hold values from -3 to 3
- dec_weight: bfloat16 [4, 20480, 2, 1024], P('layer', 'feat'), may hold values from -0.0390625 to 0.0390625
- dec_bias: float32 [4, 1024], P('layer'), may hold values from -3 to 3
Outputs:
- errors: float32 [4, 768, 1024], P('layer', 'feat')
- enc_grad: bfloat16 [4, 1024, 20480], P('layer', None, 'feat')
The draws below stay inside these ranges and needn't reach their ends.
All inputs are finite; a program needn't handle non-finite values.
Results may differ from the reference program's by a relative error of at most 0.006.
Values may be sent and summed in bfloat16 or wider, within the bound.
A program may use at most 128 MiB of HBM per device.

```python
import jax
import jax.numpy as jnp
from jax import lax

D = 1024
F = 20480
TOK = 768
LAYERS = 4


def block_levels(stream_key, extent, pieces, low, high):
    def one(axis_at, blocks):
        heights = jax.random.uniform(jax.random.fold_in(jax.random.fold_in(stream_key, 6), axis_at), (blocks,), jnp.float32, low / len(pieces), high / len(pieces))
        return jnp.repeat(jnp.exp(heights), extent[axis_at] // blocks).reshape((-1,) + (1,) * (len(extent) - axis_at - 1))

    gain = one(*pieces[0])
    for cut in pieces[1:]:
        gain = gain * one(*cut)
    return gain


def gaussian(key, dims, width, bound, pieces=(), kind=jnp.bfloat16):
    array = width * jax.random.normal(key, dims, jnp.float32)
    if pieces:
        array = array * block_levels(key, dims, pieces, -0.22, 0.18)
    return jnp.clip(array, -bound, bound).astype(kind)


def setup_inputs(seed: int = 0) -> dict:
    arg_keys = jax.random.split(jax.random.key(seed), 7)
    acts = gaussian(arg_keys[0], (LAYERS, TOK, D), 1.0, 6.0, ((0, 4),))
    targets = gaussian(arg_keys[1], (LAYERS, TOK, D), 1.0, 6.0, ((0, 4), (1, 8)))
    enc_weight = gaussian(arg_keys[2], (LAYERS, D, F), D ** -0.5, 0.1875, ((0, 4), (2, 8)))
    enc_bias = gaussian(arg_keys[3], (LAYERS, F), 0.5, 3.0, ((0, 4), (1, 8)), jnp.float32)
    dec_weight = gaussian(arg_keys[4], (LAYERS, F, 2, D), F ** -0.5, 0.0390625, ((0, 4), (1, 8)))
    dec_bias = gaussian(arg_keys[5], (LAYERS, D), 0.5, 3.0, ((0, 4),), jnp.float32)
    return {"acts": acts, "targets": targets, "enc_weight": enc_weight, "enc_bias": enc_bias, "dec_weight": dec_weight, "dec_bias": dec_bias}


def forward_layer(item):
    inputs, weight, bias, decoder = item
    pre = jnp.dot(inputs, weight, preferred_element_type=jnp.float32) + bias
    latent = (jax.nn.softplus(4.0 * pre) * 0.25).astype(jnp.bfloat16)
    own = jnp.dot(latent, decoder[:, 0, :], preferred_element_type=jnp.float32)
    later = jnp.dot(latent, decoder[:, 1, :], preferred_element_type=jnp.float32)
    return pre, own, later


def reference(acts, targets, enc_weight, enc_bias, dec_weight, dec_bias):
    pres, owns, laters = lax.map(forward_layer, (acts, enc_weight, enc_bias, dec_weight))
    carried = jnp.concatenate([jnp.zeros_like(laters[:1]), laters[:-1]], axis=0)
    errors = owns + carried + dec_bias[:, None, :] - targets.astype(jnp.float32)
    err_half = errors.astype(jnp.bfloat16)
    following = jnp.concatenate([err_half[1:], jnp.zeros_like(err_half[:1])], axis=0)
    scale = acts.shape[1] ** -0.5

    def backward_layer(item):
        inputs, pre, decoder, first, second = item
        grad_latent = lax.dot_general(first, decoder[:, 0, :], (((1,), (1,)), ((), ())), preferred_element_type=jnp.float32)
        grad_latent = grad_latent + lax.dot_general(second, decoder[:, 1, :], (((1,), (1,)), ((), ())), preferred_element_type=jnp.float32)
        grad_pre = (grad_latent * jax.nn.sigmoid(4.0 * pre)).astype(jnp.bfloat16)
        total = lax.dot_general(inputs, grad_pre, (((0,), (0,)), ((), ())), preferred_element_type=jnp.float32)
        return (total * scale).astype(jnp.bfloat16)

    enc_grad = lax.map(backward_layer, (acts, pres, dec_weight, err_half, following))
    return errors, enc_grad
```

```python
import functools

import jax
import jax.numpy as jnp
from jax import lax
from jax.experimental import pallas as pl
from jax.experimental.pallas import tpu as pltpu
from jax.sharding import PartitionSpec as P

MESH = pl.DeviceIdType.MESH
CHUNKS = 4


def exchange_kernel(
    layers, n, latent_ref, dec_ref, targets_ref, bias_ref,
    errors_ref, gath_ref, foll_ref,
    dec, later, arrived, sums, parts,
    dec_sem, up_send, up_recv, rs_send, rs_recv, ag_send, ag_recv, down_send, down_recv,
):
    layer = lax.axis_index("layer")
    me = lax.axis_index("feat")
    above = lax.rem(layer + 1, layers)
    below = lax.rem(layer + layers - 1, layers)
    tokens, width = gath_ref.shape
    rows = tokens // n
    wide = width // CHUNKS

    def peer(k):
        return lax.rem(me + k, n)

    def rows_of(i):
        return pl.ds(pl.multiple_of(i * rows, rows), rows)

    def cols(c):
        return pl.ds(pl.multiple_of(c * wide, wide), wide)

    def load(w, c):
        return pltpu.make_async_copy(
            dec_ref.at[w, :, cols(c)], dec.at[w, :, cols(c)], dec_sem.at[w, c]
        )

    def remote(src, dst, send, recv, where):
        return pltpu.make_async_remote_copy(
            src_ref=src, dst_ref=dst, send_sem=send, recv_sem=recv,
            device_id=where, device_id_type=MESH,
        )

    def up(c):
        return remote(later.at[:, cols(c)], arrived.at[:, cols(c)], up_send.at[c], up_recv.at[c], (above, me))

    def scatter(c, k):
        to = peer(k)
        return remote(
            sums.at[rows_of(to), cols(c)], parts.at[k - 1, :, cols(c)],
            rs_send.at[c, k - 1], rs_recv.at[c, k - 1], (layer, to),
        )

    def gather(c, k, owner):
        spot = gath_ref.at[rows_of(owner), cols(c)]
        return remote(spot, spot, ag_send.at[c, k - 1], ag_recv.at[c, k - 1], (layer, peer(k)))

    def down(c, k, owner):
        return remote(
            gath_ref.at[rows_of(owner), cols(c)], foll_ref.at[rows_of(owner), cols(c)],
            down_send.at[c, k], down_recv.at[c, k], (below, me),
        )

    for w in (1, 0):
        for c in range(CHUNKS):
            load(w, c).start()

    barrier = pltpu.get_barrier_semaphore()
    for k in range(1, n):
        pl.semaphore_signal(barrier, inc=1, device_id=(layer, peer(k)), device_id_type=MESH)
    pl.semaphore_signal(barrier, inc=1, device_id=(above, me), device_id_type=MESH)
    pl.semaphore_signal(barrier, inc=1, device_id=(below, me), device_id_type=MESH)
    pl.semaphore_wait(barrier, n + 1)

    @pl.loop(0, CHUNKS)
    def _(c):
        load(1, c).wait()
        later[:, cols(c)] = jnp.dot(
            latent_ref[...], dec[1, :, cols(c)], preferred_element_type=jnp.float32
        ).astype(jnp.bfloat16)
        up(c).start()

    @pl.loop(0, CHUNKS)
    def _(c):
        load(0, c).wait()
        own = jnp.dot(latent_ref[...], dec[0, :, cols(c)], preferred_element_type=jnp.float32)
        up(c).wait_recv()
        carried = jnp.where(layer > 0, arrived[:, cols(c)].astype(jnp.float32), 0.0)
        sums[:, cols(c)] = (own + carried).astype(jnp.bfloat16)
        for k in range(1, n):
            scatter(c, k).start()

    @pl.loop(0, CHUNKS)
    def _(c):
        total = sums[rows_of(me), cols(c)].astype(jnp.float32)
        for k in range(1, n):
            scatter(c, k).wait_recv()
            total = total + parts[k - 1, :, cols(c)].astype(jnp.float32)
        errors = total + bias_ref[:, cols(c)] - targets_ref[:, cols(c)].astype(jnp.float32)
        errors_ref[:, cols(c)] = errors
        gath_ref[rows_of(me), cols(c)] = errors.astype(jnp.bfloat16)
        for k in range(1, n):
            gather(c, k, me).start()
        down(c, 0, me).start()

    @pl.loop(0, CHUNKS)
    def _(c):
        for k in range(1, n):
            owner = lax.rem(me + n - k, n)
            gather(c, k, owner).wait_recv()
            down(c, k, owner).start()

    @pl.loop(0, CHUNKS)
    def _(c):
        up(c).wait_send()
        for k in range(1, n):
            scatter(c, k).wait_send()
            gather(c, k, me).wait_send()
        for k in range(n):
            owner = lax.rem(me + n - k, n)
            down(c, k, owner).wait_recv()
            down(c, k, owner).wait_send()

    @pl.when(layer == layers - 1)
    def _():
        foll_ref[...] = jnp.zeros_like(foll_ref)


def exchange(layers, n, latent, dec, targets, bias):
    tokens, features = latent.shape
    width = dec.shape[2]
    rows = tokens // n
    half = jnp.bfloat16
    vmem = pl.BlockSpec(memory_space=pltpu.VMEM)
    dma = pltpu.SemaphoreType.DMA
    return pl.pallas_call(
        functools.partial(exchange_kernel, layers, n),
        out_shape=(
            jax.ShapeDtypeStruct((rows, width), jnp.float32),
            jax.ShapeDtypeStruct((tokens, width), half),
            jax.ShapeDtypeStruct((tokens, width), half),
        ),
        in_specs=[vmem, pl.BlockSpec(memory_space=pl.ANY), vmem, vmem],
        out_specs=(vmem, vmem, vmem),
        scratch_shapes=[
            pltpu.VMEM((2, features, width), half),
            pltpu.VMEM((tokens, width), half),
            pltpu.VMEM((tokens, width), half),
            pltpu.VMEM((tokens, width), half),
            pltpu.VMEM((n - 1, rows, width), half),
            dma((2, CHUNKS)),
            dma((CHUNKS,)),
            dma((CHUNKS,)),
            dma((CHUNKS, n - 1)),
            dma((CHUNKS, n - 1)),
            dma((CHUNKS, n - 1)),
            dma((CHUNKS, n - 1)),
            dma((CHUNKS, n)),
            dma((CHUNKS, n)),
        ],
        compiler_params=pltpu.CompilerParams(
            collective_id=0, has_side_effects=True, vmem_limit_bytes=48 * 2**20
        ),
        name="exchange",
    )(latent, dec, targets, bias)


def contract_width(errs, decoder):
    return lax.dot_general(
        errs, decoder, (((1,), (1,)), ((), ())), preferred_element_type=jnp.float32
    )


def local(layers, n, acts, targets, enc_weight, enc_bias, dec_weight, dec_bias):
    inputs = acts[0]
    weight = enc_weight[0]
    bias = enc_bias[0]
    dec = jnp.transpose(dec_weight[0], (1, 0, 2))
    tokens = inputs.shape[0]
    pre = jnp.dot(inputs, weight, preferred_element_type=jnp.float32) + bias
    latent = (jax.nn.softplus(4.0 * pre) * 0.25).astype(jnp.bfloat16)
    errors, gathered, following = exchange(layers, n, latent, dec, targets[0], dec_bias)
    deriv = jax.nn.sigmoid(4.0 * pre)
    scale = tokens ** (-0.5)
    grad_latent = contract_width(gathered, dec[0]) + contract_width(following, dec[1])
    grad_pre = (grad_latent * deriv).astype(jnp.bfloat16)
    total = lax.dot_general(
        inputs, grad_pre, (((0,), (0,)), ((), ())), preferred_element_type=jnp.float32
    )
    enc_grad = (total * scale).astype(jnp.bfloat16)
    return (errors[None], enc_grad[None])


def solution(mesh):
    return jax.shard_map(
        functools.partial(local, mesh.shape["layer"], mesh.shape["feat"]),
        mesh=mesh,
        in_specs=(
            P("layer", None, None),
            P("layer", "feat", None),
            P("layer", None, "feat"),
            P("layer", "feat"),
            P("layer", "feat", None, None),
            P("layer", None),
        ),
        out_specs=(P("layer", "feat", None), P("layer", None, "feat")),
        check_vma=False,
    )
```

```python
import functools

import jax
import jax.numpy as jnp
from jax import lax
from jax.experimental import pallas as pl
from jax.experimental.pallas import tpu as pltpu
from jax.sharding import PartitionSpec as P

MESH = pl.DeviceIdType.MESH
CHUNKS = 4


def inner_of(n):
    return max(d for d in range(1, n + 1) if n % d == 0 and d * d <= n)


def exchange_kernel(
    layers, m, o, latent_ref, dec_ref, targets_ref, bias_ref, acts_ref,
    errors_ref, gath_ref, foll_ref, turned_ref,
    dec, later, arrived, sums, near, mids, far, mine,
    dec_sem, up_send, up_recv, near_send, near_recv, far_send, far_recv,
    out_send, out_recv, in_send, in_recv, down_send, down_recv,
):
    layer = lax.axis_index("layer")
    me = lax.axis_index("feat")
    z, x = me // m, lax.rem(me, m)
    above = lax.rem(layer + 1, layers)
    below = lax.rem(layer + layers - 1, layers)
    tokens, width = gath_ref.shape
    rows = tokens // (m * o)
    wide = width // CHUNKS

    def at(dz, dx):
        return lax.rem(z + dz + o, o) * m + lax.rem(x + dx + m, m)

    def rows_of(i):
        return pl.ds(pl.multiple_of(i * rows, rows), rows)

    def cols(c):
        return pl.ds(pl.multiple_of(c * wide, wide), wide)

    def load(w, c):
        return pltpu.make_async_copy(
            dec_ref.at[w, :, cols(c)], dec.at[w, :, cols(c)], dec_sem.at[w, c]
        )

    def remote(src, dst, send, recv, where):
        return pltpu.make_async_remote_copy(
            src_ref=src, dst_ref=dst, send_sem=send, recv_sem=recv,
            device_id=where, device_id_type=MESH,
        )

    def up(c):
        return remote(later.at[:, cols(c)], arrived.at[:, cols(c)], up_send.at[c], up_recv.at[c], (above, me))

    def add_near(c, q, r):
        j = (q - 1) * o + r
        return remote(
            sums.at[rows_of(at(r, q)), cols(c)], near.at[j, :, cols(c)],
            near_send.at[c, j], near_recv.at[c, j], (layer, at(0, q)),
        )

    def add_far(c, r):
        return remote(
            mids.at[r - 1, :, cols(c)], far.at[r - 1, :, cols(c)],
            far_send.at[c, r - 1], far_recv.at[c, r - 1], (layer, at(r, 0)),
        )

    def give_far(c, r, owner):
        spot = gath_ref.at[rows_of(owner), cols(c)]
        return remote(spot, spot, out_send.at[c, r - 1], out_recv.at[c, r - 1], (layer, at(r, 0)))

    def give_near(c, q, r, owner):
        j = (q - 1) * o + r
        spot = gath_ref.at[rows_of(owner), cols(c)]
        return remote(spot, spot, in_send.at[c, j], in_recv.at[c, j], (layer, at(0, q)))

    def down(c, q, r):
        owner = at(-r, -q)
        j = q * o + r
        return remote(
            gath_ref.at[rows_of(owner), cols(c)], foll_ref.at[rows_of(owner), cols(c)],
            down_send.at[c, j], down_recv.at[c, j], (below, me),
        )

    for w in (1, 0):
        for c in range(CHUNKS):
            load(w, c).start()

    barrier = pltpu.get_barrier_semaphore()
    for to in (
        [(layer, at(0, q)) for q in range(1, m)]
        + [(layer, at(r, 0)) for r in range(1, o)]
        + [(above, me), (below, me)]
    ):
        pl.semaphore_signal(barrier, inc=1, device_id=to, device_id_type=MESH)
    pl.semaphore_wait(barrier, m + o)

    @pl.loop(0, CHUNKS)
    def _(c):
        load(1, c).wait()
        later[:, cols(c)] = jnp.dot(
            latent_ref[...], dec[1, :, cols(c)], preferred_element_type=jnp.float32
        ).astype(jnp.bfloat16)
        up(c).start()

    @pl.loop(0, CHUNKS)
    def _(c):
        load(0, c).wait()
        own = jnp.dot(latent_ref[...], dec[0, :, cols(c)], preferred_element_type=jnp.float32)
        up(c).wait_recv()
        carried = jnp.where(layer > 0, arrived[:, cols(c)].astype(jnp.float32), 0.0)
        sums[:, cols(c)] = (own + carried).astype(jnp.bfloat16)
        for q in range(1, m):
            for r in range(o):
                add_near(c, q, r).start()

    turned_ref[...] = acts_ref[...].T

    @pl.loop(0, CHUNKS)
    def _(c):
        for r in (*range(1, o), 0):
            total = sums[rows_of(at(r, 0)), cols(c)].astype(jnp.float32)
            for q in range(1, m):
                add_near(c, q, r).wait_recv()
                total = total + near[(q - 1) * o + r, :, cols(c)].astype(jnp.float32)
            if r:
                mids[r - 1, :, cols(c)] = total.astype(jnp.bfloat16)
                add_far(c, r).start()
            else:
                mine[:, cols(c)] = total

    @pl.loop(0, CHUNKS)
    def _(c):
        total = mine[:, cols(c)]
        for r in range(1, o):
            add_far(c, r).wait_recv()
            total = total + far[r - 1, :, cols(c)].astype(jnp.float32)
        errors = total + bias_ref[:, cols(c)] - targets_ref[:, cols(c)].astype(jnp.float32)
        errors_ref[:, cols(c)] = errors
        gath_ref[rows_of(me), cols(c)] = errors.astype(jnp.bfloat16)
        for r in range(1, o):
            give_far(c, r, me).start()
        for q in range(1, m):
            give_near(c, q, 0, me).start()
        down(c, 0, 0).start()

    @pl.loop(0, CHUNKS)
    def _(c):
        for r in range(1, o):
            owner = at(-r, 0)
            give_far(c, r, owner).wait_recv()
            for q in range(1, m):
                give_near(c, q, r, owner).start()
            down(c, 0, r).start()

    @pl.loop(0, CHUNKS)
    def _(c):
        for q in range(1, m):
            for r in range(o):
                give_near(c, q, r, at(-r, -q)).wait_recv()
                down(c, q, r).start()

    @pl.loop(0, CHUNKS)
    def _(c):
        up(c).wait_send()
        for r in range(1, o):
            add_far(c, r).wait_send()
            give_far(c, r, me).wait_send()
        for r in range(o):
            for q in range(1, m):
                add_near(c, q, r).wait_send()
                give_near(c, q, r, at(-r, 0)).wait_send()
            for q in range(m):
                down(c, q, r).wait_recv()
                down(c, q, r).wait_send()

    @pl.when(layer == layers - 1)
    def _():
        foll_ref[...] = jnp.zeros_like(foll_ref)


def exchange(layers, n, latent, dec, targets, bias, acts):
    tokens, features = latent.shape
    width = dec.shape[2]
    rows = tokens // n
    m = inner_of(n)
    o = n // m
    half = jnp.bfloat16
    vmem = pl.BlockSpec(memory_space=pltpu.VMEM)
    dma = pltpu.SemaphoreType.DMA
    pairs = [(CHUNKS, k) for k in ((m - 1) * o, o - 1, o - 1, (m - 1) * o, n)]
    return pl.pallas_call(
        functools.partial(exchange_kernel, layers, m, o),
        out_shape=(
            jax.ShapeDtypeStruct((rows, width), jnp.float32),
            jax.ShapeDtypeStruct((tokens, width), half),
            jax.ShapeDtypeStruct((tokens, width), half),
            jax.ShapeDtypeStruct((width, tokens), half),
        ),
        in_specs=[vmem, pl.BlockSpec(memory_space=pl.ANY), vmem, vmem, vmem],
        out_specs=(vmem, vmem, vmem, vmem),
        scratch_shapes=[
            pltpu.VMEM((2, features, width), half),
            pltpu.VMEM((tokens, width), half),
            pltpu.VMEM((tokens, width), half),
            pltpu.VMEM((tokens, width), half),
            pltpu.VMEM(((m - 1) * o, rows, width), half),
            pltpu.VMEM((o - 1, rows, width), half),
            pltpu.VMEM((o - 1, rows, width), half),
            pltpu.VMEM((rows, width), jnp.float32),
            dma((2, CHUNKS)),
            dma((CHUNKS,)),
            dma((CHUNKS,)),
            *[dma(p) for p in pairs for _ in range(2)],
        ],
        compiler_params=pltpu.CompilerParams(
            collective_id=0, has_side_effects=True, vmem_limit_bytes=48 * 2**20
        ),
        name="exchange",
    )(latent, dec, targets, bias, acts)


def grad_kernel(scale, gath_ref, foll_ref, turned_ref, dec_ref, pre_ref, out_ref):
    grad_latent = contract_width(gath_ref[...], dec_ref[0]) + contract_width(foll_ref[...], dec_ref[1])
    deriv = jax.nn.sigmoid(4.0 * pre_ref[...])
    grad_pre = (grad_latent * deriv).astype(jnp.bfloat16)
    total = jnp.dot(turned_ref[...], grad_pre, preferred_element_type=jnp.float32)
    out_ref[...] = (total * scale).astype(jnp.bfloat16)


def encoder_grad(gathered, following, turned, dec, pre):
    tokens, features = pre.shape
    width = turned.shape[0]
    tile = 256
    vmem = pl.BlockSpec(memory_space=pltpu.VMEM)
    return pl.pallas_call(
        functools.partial(grad_kernel, tokens ** (-0.5)),
        grid=(features // tile,),
        out_shape=jax.ShapeDtypeStruct((width, features), jnp.bfloat16),
        in_specs=[
            vmem, vmem, vmem,
            pl.BlockSpec((2, tile, width), lambda i: (0, i, 0)),
            pl.BlockSpec((tokens, tile), lambda i: (0, i)),
        ],
        out_specs=pl.BlockSpec((width, tile), lambda i: (0, i)),
        compiler_params=pltpu.CompilerParams(vmem_limit_bytes=40 * 2**20),
        name="encoder_grad",
    )(gathered, following, turned, dec, pre)


def contract_width(errs, decoder):
    return lax.dot_general(
        errs, decoder, (((1,), (1,)), ((), ())), preferred_element_type=jnp.float32
    )


def local(layers, n, acts, targets, enc_weight, enc_bias, dec_weight, dec_bias):
    inputs = acts[0]
    weight = enc_weight[0]
    bias = enc_bias[0]
    dec = jnp.transpose(dec_weight[0], (1, 0, 2))
    pre = jnp.dot(inputs, weight, preferred_element_type=jnp.float32) + bias
    latent = (jax.nn.softplus(4.0 * pre) * 0.25).astype(jnp.bfloat16)
    errors, gathered, following, turned = exchange(
        layers, n, latent, dec, targets[0], dec_bias, inputs
    )
    enc_grad = encoder_grad(gathered, following, turned, dec, pre)
    return (errors[None], enc_grad[None])


def solution(mesh):
    return jax.shard_map(
        functools.partial(local, mesh.shape["layer"], mesh.shape["feat"]),
        mesh=mesh,
        in_specs=(
            P("layer", None, None),
            P("layer", "feat", None),
            P("layer", None, "feat"),
            P("layer", "feat"),
            P("layer", "feat", None, None),
            P("layer", None),
        ),
        out_specs=(P("layer", "feat", None), P("layer", None, "feat")),
        check_vma=False,
    )
```
